256 devices in a mesh: own: 32 (over y, x, core), row: 8 (over z).
Axes of the slice: x: 4, y: 4, z: 8, core: 2. Of those that a mesh axis runs over, the one named last changes fastest.
Arguments:
- weights: float32 [32, 8, 128, 2048], P('own', None, 'row'), may hold values from -200 to 200
- first_moment: float32 [32, 8, 128, 2048], P('own', None, 'row'), may hold values from -20 to 20
- second_moment: float32 [32, 8, 128, 2048], P('own', None, 'row'), may hold values from 0.002 to 0.05
- gradient: bfloat16 [32, 8, 128, 2048], P('own', None, 'row'), may hold values from -0.59765625 to 0.59765625
- owner: int32 [127], replicated, may hold values from 0 to 31, as said below
Outputs:
- new_weights: float32 [32, 8, 128, 2048], P('own', None, 'row')
- new_first: float32 [32, 8, 128, 2048], P('own', None, 'row')
- new_second: float32 [32, 8, 128, 2048], P('own', None, 'row')
- low_weights: bfloat16 [32, 8, 128, 2048], P('own')
- weight_norms: float32 [14], replicated
- update_norms: float32 [14], replicated
- trust_ratios: float32 [14], replicated
The draws below stay inside these ranges and needn't reach their ends.
Inputs may be any that keep to these rules, and one draw needn't show every extreme that they name: No owner group holds more than 8 tiles, and one holds exactly 8.
All inputs are finite; a program needn't handle non-finite values.
Results may differ from the reference program's by a relative error of at most 0.0004.
Values may be sent and summed in bfloat16 or wider, within the bound.
A program may use at most 128 MiB of HBM per device.

```python
import math
import jax
import jax.numpy as jnp
import numpy as np
from jax import lax

D = 2048
QW = 4096
KVW = 512
NEXP = 128
FF = 768
EW = 3
TILE = 128
TILES = 127
CAP = 8
MATS = 14
N_OWN = 32


def scaled_field(base_key, factor):
    key_base, key_rows, key_cols = jax.random.split(base_key, 3)
    shape = (N_OWN, CAP, TILE, D)
    base_field = jnp.clip(jax.random.normal(key_base, shape, jnp.float32), -6.0, 6.0)
    row_scale = jnp.exp(jax.random.uniform(key_rows, (N_OWN, CAP, TILE, 1), jnp.float32, -1.15, 1.15))
    col_scale = jnp.exp(jax.random.uniform(key_cols, (N_OWN, CAP, 1, D), jnp.float32, -1.15, 1.15))
    rise_factor = 1.0 + 2.0 * jnp.arange(TILE, dtype=jnp.float32).reshape(1, 1, TILE, 1) / (TILE - 1)
    return factor * base_field * row_scale * col_scale * rise_factor


def draw_weights(key, part):
    return scaled_field(jax.random.fold_in(key, 11), 1.0)


def draw_first_moment(key, part):
    return scaled_field(jax.random.fold_in(key, 23), 0.1)


def draw_owner(key, part):
    key_perm, key_pick, key_rest = jax.random.split(jax.random.fold_in(key, 37), 3)
    tile_order = jax.random.permutation(key_perm, TILES)
    busiest = jax.random.randint(key_pick, (), 0, N_OWN)
    others = jax.random.permutation(key_rest, N_OWN - 1)
    others = others + (others >= busiest).astype(jnp.int32)
    position = jnp.arange(TILES, dtype=jnp.int32)
    placed = jnp.where(position < CAP, busiest, others[(position - CAP) % (N_OWN - 1)])
    return jnp.zeros((TILES,), jnp.int32).at[tile_order].set(placed.astype(jnp.int32))


def levels(key, shape, cuts, smallest, high):
    def one(dim, shards_of):
        steps = jax.random.uniform(jax.random.fold_in(jax.random.fold_in(key, 6), dim), (shards_of,), jnp.float32, smallest / len(cuts), high / len(cuts))
        return jnp.repeat(jnp.exp(steps), shape[dim] // shards_of).reshape((-1,) + (1,) * (len(shape) - dim - 1))

    gain = one(*cuts[0])
    for cut in cuts[1:]:
        gain = gain * one(*cut)
    return gain


def noise(key, dims, spread, bound, cuts=(), held_as=jnp.bfloat16):
    loudness = levels(key, dims, cuts, -0.22, 0.18) if cuts else 1.0
    drawn = jax.random.normal(key, dims, jnp.float32) * spread * loudness
    return jnp.minimum(jnp.maximum(drawn, -bound), bound).astype(held_as)


def setup_inputs(seed: int = 0) -> dict:
    key_list = jax.random.split(jax.random.key(seed), 6)
    return {
        "weights": draw_weights(jax.random.fold_in(key_list[5], 71), 0),
        "first_moment": draw_first_moment(jax.random.fold_in(key_list[5], 71), 0),
        "second_moment": jnp.clip(jnp.exp(math.log(0.05) - 3.218876 * jax.random.uniform(key_list[2], (N_OWN, CAP, TILE, D), jnp.float32) ** levels(key_list[2], (N_OWN, CAP, TILE, D), ((0, 32), (2, 8)), -0.2, 0.2)), 0.002, 0.05),
        "gradient": noise(key_list[3], (N_OWN, CAP, TILE, D), 0.1, 0.59765625, ((0, 32), (2, 8))),
        "owner": draw_owner(jax.random.fold_in(key_list[5], 71), 0),
    }


DECAY = 0.1
STEP_SIZE = 0.05
EPSILON = 1e-06

def matrix_table():
    counts = [QW // TILE, KVW // TILE, KVW // TILE, QW // TILE, NEXP // TILE] + [FF // TILE] * (3 * EW)
    return np.repeat(np.arange(len(counts)), counts).astype(np.int32)

def slot_select(owner, owners_count, slot_count, matrices):
    tile_table = jnp.asarray(matrix_table())
    owner_hit = (owner[:, None] == jnp.arange(owners_count, dtype=jnp.int32)[None, :]).astype(jnp.int32)
    tile_rank = lax.optimization_barrier(jnp.sum((jnp.cumsum(owner_hit, 0) - owner_hit) * owner_hit, 1))
    slot_hit = tile_rank[:, None] == jnp.arange(slot_count, dtype=jnp.int32)[None, :]
    matrix_hit = tile_table[:, None] == jnp.arange(matrices, dtype=jnp.int32)[None, :]
    owner_bool = owner_hit > 0
    joined = owner_bool[:, :, None, None] & slot_hit[:, None, :, None] & matrix_hit[:, None, None, :]
    return jnp.any(joined, axis=0).astype(jnp.float32)

def reference(weights, first_moment, second_moment, gradient, owner):
    select = slot_select(owner, N_OWN, CAP, MATS)
    used = lax.optimization_barrier(jnp.sum(select, 2))[:, :, None, None]
    grad_wide = gradient.astype(jnp.float32)
    moment_one = 0.5 * first_moment + 0.5 * grad_wide
    moment_two = 0.5 * second_moment + 0.5 * grad_wide * grad_wide
    direction = moment_one / (jnp.sqrt(moment_two) + EPSILON) + DECAY * weights
    weight_sq = lax.optimization_barrier(jnp.sum(weights * weights, axis=(2, 3)))
    update_sq = lax.optimization_barrier(jnp.sum(direction * direction, axis=(2, 3)))
    weight_norms = jnp.sqrt(lax.optimization_barrier(jnp.sum(select * weight_sq[:, :, None], axis=(0, 1))))
    update_norms = jnp.sqrt(lax.optimization_barrier(jnp.sum(select * update_sq[:, :, None], axis=(0, 1))))
    trust_ratios = weight_norms / (update_norms + EPSILON)
    slot_ratio = lax.optimization_barrier(jnp.sum(select * trust_ratios[None, None, :], 2))[:, :, None, None]
    new_weights = used * (weights - STEP_SIZE * slot_ratio * direction)
    new_first = used * moment_one
    new_second = used * moment_two
    low_weights = new_weights.astype(jnp.bfloat16)
    return (new_weights, new_first, new_second, low_weights, weight_norms, update_norms, trust_ratios)
```

```python
import functools

import jax
import jax.numpy as jnp
import numpy as np
from jax import lax
from jax.experimental import pallas as pl
from jax.experimental.pallas import tpu as pltpu
from jax.sharding import PartitionSpec as P

QW = 4096
KVW = 512
NEXP = 128
FF = 768
EW = 3
TILE = 128
MATS = 14

DECAY = 0.1
STEP_SIZE = 0.05
EPSILON = 1e-06

MESH = pl.DeviceIdType.MESH
HALF = 64
CHUNK = 512


def matrix_bounds():
    counts = [QW // TILE, KVW // TILE, KVW // TILE, QW // TILE, NEXP // TILE] + [FF // TILE] * (
        3 * EW
    )
    ends = np.cumsum(counts)
    return [(int(e - c), int(e)) for c, e in zip(counts, ends)]


def select_rows(owner, me, slots):
    tiles = owner.shape[1]
    hit = jnp.broadcast_to((owner == me).astype(jnp.float32), (8, tiles))
    before = (
        lax.broadcasted_iota(jnp.int32, (tiles, tiles), 0)
        < lax.broadcasted_iota(jnp.int32, (tiles, tiles), 1)
    ).astype(jnp.float32)
    rank = jnp.dot(hit, before, preferred_element_type=jnp.float32)
    slot = lax.broadcasted_iota(jnp.int32, (slots, tiles), 0).astype(jnp.float32)
    slot_hit = jnp.where(rank == slot, hit, 0.0)
    lane = lax.broadcasted_iota(jnp.int32, (1, 128), 1) % HALF
    first = jnp.full((1, 128), 1 << 20, jnp.int32)
    last = jnp.zeros((1, 128), jnp.int32)
    for k, (a, b) in enumerate(matrix_bounds()):
        first = jnp.where(lane == k, a, first)
        last = jnp.where(lane == k, b, last)
    tile = lax.broadcasted_iota(jnp.int32, (tiles, 128), 0)
    table = ((tile >= first) & (tile < last)).astype(jnp.float32)
    return jnp.dot(slot_hit, table, preferred_element_type=jnp.float32)


def fold(x):
    x = x[0:8, :] + x[8:16, :]
    out = x[:, 0:128]
    for i in range(1, CHUNK // 128):
        out = out + x[:, i * 128 : (i + 1) * 128]
    return out


def kernel(
    owns, rows,
    w_hbm, f_hbm, s_hbm, g_hbm, owner_ref,
    nw_hbm, nf_hbm, ns_hbm, low_hbm, wn_ref, un_ref, tr_ref,
    wv, fv, sv, gv, dv, gath, used_b, ratio_b, sw, su, abuf, bbuf,
    in_sem, out_sem, gat_sem, a_sem, b_sem, rs_sem, rr_sem, ls_sem, lr_sem,
):
    own = lax.axis_index("own")
    z = lax.axis_index("row")
    slots, depth, width = wv.shape

    barrier = pltpu.get_barrier_semaphore()

    @pl.loop(1, owns)
    def _(p):
        pl.semaphore_signal(barrier, inc=1, device_id=(lax.rem(own + p, owns), z), device_id_type=MESH)

    @pl.loop(1, rows)
    def _(p):
        pl.semaphore_signal(barrier, inc=1, device_id=(own, lax.rem(z + p, rows)), device_id_type=MESH)

    def loads(c):
        return [
            pltpu.make_async_copy(src.at[0, c], dst.at[c], in_sem.at[i, c])
            for i, (src, dst) in enumerate(((w_hbm, wv), (f_hbm, fv), (s_hbm, sv), (g_hbm, gv)))
        ]

    @pl.loop(0, slots)
    def _(c):
        for copy in loads(c):
            copy.start()

    select = select_rows(owner_ref[...], own, slots)
    lane = lax.broadcasted_iota(jnp.int32, (1, 128), 1)
    lower = lane < HALF
    used = jnp.sum(jnp.where(lower, select, 0.0), axis=1, keepdims=True)
    used_b[...] = jnp.broadcast_to(used, used_b.shape)

    def stores(c):
        return [
            pltpu.make_async_copy(fv.at[c], nf_hbm.at[0, c], out_sem.at[0, c]),
            pltpu.make_async_copy(sv.at[c], ns_hbm.at[0, c], out_sem.at[1, c]),
        ]

    @pl.loop(0, slots)
    def _(c):
        for copy in loads(c):
            copy.wait()
        keep = used_b[pl.ds(c, 1), :]
        aw = jnp.zeros((8, 128), jnp.float32)
        au = jnp.zeros((8, 128), jnp.float32)
        for j in range(width // CHUNK):
            cols = slice(j * CHUNK, (j + 1) * CHUNK)
            w = wv[c, :, cols]
            g = gv[c, :, cols].astype(jnp.float32)
            m1 = 0.5 * fv[c, :, cols] + 0.5 * g
            m2 = 0.5 * sv[c, :, cols] + 0.5 * g * g
            d = m1 / (jnp.sqrt(m2) + EPSILON) + DECAY * w
            fv[c, :, cols] = keep * m1
            sv[c, :, cols] = keep * m2
            dv[c, :, cols] = d
            aw = aw + fold(w * w)
            au = au + fold(d * d)
        sw[c] = aw
        su[c] = au
        for copy in stores(c):
            copy.start()

    weight_sq = jnp.sum(jnp.sum(sw[...], axis=1), axis=1, keepdims=True)
    update_sq = jnp.sum(jnp.sum(su[...], axis=1), axis=1, keepdims=True)
    part = jnp.sum(select * jnp.where(lower, weight_sq, update_sq), axis=0, keepdims=True)
    abuf[pl.ds(own, 1)] = part.reshape(1, 1, 128)

    pl.semaphore_wait(barrier, owns + rows - 2)

    def plane(p):
        return pltpu.make_async_remote_copy(
            src_ref=abuf.at[own], dst_ref=abuf.at[own],
            send_sem=a_sem.at[0], recv_sem=a_sem.at[1],
            device_id=(lax.rem(own + p, owns), z), device_id_type=MESH,
        )

    def line(p):
        return pltpu.make_async_remote_copy(
            src_ref=bbuf.at[z], dst_ref=bbuf.at[z],
            send_sem=b_sem.at[0], recv_sem=b_sem.at[1],
            device_id=(own, lax.rem(z + p, rows)), device_id_type=MESH,
        )

    @pl.loop(1, owns)
    def _(p):
        plane(p).start()

    whole = abuf.at[pl.ds(0, owns - 1)]
    pltpu.make_async_copy(whole, whole, a_sem.at[1]).wait()
    total = jnp.sum(abuf[...], axis=0)
    bbuf[pl.ds(z, 1)] = total.reshape(1, 1, 128)
    pltpu.make_async_copy(whole, whole, a_sem.at[0]).wait()

    @pl.loop(1, rows)
    def _(p):
        line(p).start()

    whole_b = bbuf.at[pl.ds(0, rows - 1)]
    pltpu.make_async_copy(whole_b, whole_b, b_sem.at[1]).wait()
    norms = jnp.sqrt(jnp.sum(bbuf[...], axis=0))
    updates = pltpu.roll(norms, HALF, 1)
    trust = norms / (updates + EPSILON)
    wn_ref[...] = norms[:, :MATS]
    un_ref[...] = updates[:, :MATS]
    tr_ref[...] = trust[:, :MATS]
    ratio = jnp.sum(jnp.where(lower, select * trust, 0.0), axis=1, keepdims=True)
    ratio_b[...] = jnp.broadcast_to(STEP_SIZE * ratio, ratio_b.shape)

    right, left = lax.rem(z + 1, rows), lax.rem(z + rows - 1, rows)

    def hop(c, h, to_right):
        src = lax.rem(z + rows - h, rows) if to_right else lax.rem(z + h, rows)
        block = gath.at[c, pl.ds(pl.multiple_of(src * depth, depth), depth)]
        send, recv = (rs_sem, rr_sem) if to_right else (ls_sem, lr_sem)
        return pltpu.make_async_remote_copy(
            src_ref=block, dst_ref=block,
            send_sem=send.at[h, c], recv_sem=recv.at[h, c],
            device_id=(own, right if to_right else left), device_id_type=MESH,
        )

    def arrival(c, h, to_right):
        src = lax.rem(z + rows - h - 1, rows) if to_right else lax.rem(z + h + 1, rows)
        block = gath.at[c, pl.ds(pl.multiple_of(src * depth, depth), depth)]
        recv = rr_sem if to_right else lr_sem
        pltpu.make_async_copy(block, block, recv.at[h, c]).wait()
        return src, block

    def keep_block(c, src, block, h, side):
        return pltpu.make_async_copy(
            block, low_hbm.at[0, c, pl.ds(pl.multiple_of(src * depth, depth), depth)], gat_sem.at[side, h, c]
        )

    mine = pl.multiple_of(z * depth, depth)

    @pl.loop(0, slots)
    def _(c):
        keep = used_b[pl.ds(c, 1), :]
        rate = ratio_b[pl.ds(c, 1), :]
        for j in range(width // CHUNK):
            cols = slice(j * CHUNK, (j + 1) * CHUNK)
            new = keep * (wv[c, :, cols] - rate * dv[c, :, cols])
            wv[c, :, cols] = new
            gath[c, pl.ds(mine, depth), cols] = new.astype(jnp.bfloat16)
        hop(c, 0, True).start()
        hop(c, 0, False).start()
        pltpu.make_async_copy(wv.at[c], nw_hbm.at[0, c], out_sem.at[2, c]).start()
        keep_block(c, z, gath.at[c, pl.ds(mine, depth)], 0, 0).start()

    half = slots // 2
    far = rows // 2
    for h in range(far):
        last = h == far - 1
        for to_right, lo, hi in ((True, 0, half if last else slots), (False, half if last else 0, slots)):
            @pl.loop(lo, hi)
            def _(c):
                src, block = arrival(c, h, to_right)
                if h + 1 < far - 1:
                    hop(c, h + 1, to_right).start()
                elif h + 1 == far - 1:
                    @pl.when((c < half) if to_right else (c >= half))
                    def _():
                        hop(c, h + 1, to_right).start()
                keep_block(c, src, block, h + 1, 0 if to_right else 1).start()

    @pl.loop(0, slots)
    def _(c):
        for copy in stores(c):
            copy.wait()
        pltpu.make_async_copy(wv.at[c], nw_hbm.at[0, c], out_sem.at[2, c]).wait()
        keep_block(c, z, gath.at[c, pl.ds(mine, depth)], 0, 0).wait()

    for h in range(far):
        last = h == far - 1
        for to_right, lo, hi in ((True, 0, half if last else slots), (False, half if last else 0, slots)):
            @pl.loop(lo, hi)
            def _(c):
                src = lax.rem(z + rows - h - 1, rows) if to_right else lax.rem(z + h + 1, rows)
                block = gath.at[c, pl.ds(pl.multiple_of(src * depth, depth), depth)]
                keep_block(c, src, block, h + 1, 0 if to_right else 1).wait()
                hop(c, h, to_right).wait_send()

    pltpu.make_async_copy(whole_b, whole_b, b_sem.at[0]).wait()


def shards(owns, rows, weights, first_moment, second_moment, gradient, owner):
    _, slots, depth, width = weights.shape
    any_space = pl.BlockSpec(memory_space=pl.ANY)
    vmem = pl.BlockSpec(memory_space=pltpu.VMEM)
    far = rows // 2
    f32 = jnp.float32
    wide = jax.ShapeDtypeStruct(weights.shape, f32)
    tiny = jax.ShapeDtypeStruct((1, MATS), f32)
    dma = pltpu.SemaphoreType.DMA
    nw, nf, ns, low, wn, un, tr = pl.pallas_call(
        functools.partial(kernel, owns, rows),
        out_shape=(
            wide, wide, wide,
            jax.ShapeDtypeStruct((1, slots, depth * rows, width), jnp.bfloat16),
            tiny, tiny, tiny,
        ),
        in_specs=[any_space] * 4 + [vmem],
        out_specs=(any_space,) * 4 + (vmem,) * 3,
        scratch_shapes=[
            pltpu.VMEM((slots, depth, width), f32),
            pltpu.VMEM((slots, depth, width), f32),
            pltpu.VMEM((slots, depth, width), f32),
            pltpu.VMEM((slots, depth, width), jnp.bfloat16),
            pltpu.VMEM((slots, depth, width), f32),
            pltpu.VMEM((slots, depth * rows, width), jnp.bfloat16),
            pltpu.VMEM((slots, CHUNK), f32),
            pltpu.VMEM((slots, CHUNK), f32),
            pltpu.VMEM((slots, 8, 128), f32),
            pltpu.VMEM((slots, 8, 128), f32),
            pltpu.VMEM((owns, 1, 128), f32),
            pltpu.VMEM((rows, 1, 128), f32),
            dma((4, slots)),
            dma((3, slots)),
            dma((2, far + 1, slots)),
            dma((2,)),
            dma((2,)),
            dma((far, slots)),
            dma((far, slots)),
            dma((far, slots)),
            dma((far, slots)),
        ],
        compiler_params=pltpu.CompilerParams(
            collective_id=0, has_side_effects=True, vmem_limit_bytes=24 << 20
        ),
    )(weights, first_moment, second_moment, gradient, owner.reshape(1, -1))
    return nw, nf, ns, low, wn.reshape(MATS), un.reshape(MATS), tr.reshape(MATS)


def solution(mesh):
    placed = P("own", None, "row", None)
    return jax.shard_map(
        functools.partial(shards, mesh.shape["own"], mesh.shape["row"]),
        mesh=mesh,
        in_specs=(placed, placed, placed, placed, P()),
        out_specs=(placed, placed, placed, P("own", None, None, None), P(), P(), P()),
        check_vma=False,
    )
```

```python
import functools

import jax
import jax.numpy as jnp
import numpy as np
from jax import lax
from jax.experimental import pallas as pl
from jax.experimental.pallas import tpu as pltpu
from jax.sharding import PartitionSpec as P

QW = 4096
KVW = 512
NEXP = 128
FF = 768
EW = 3
TILE = 128
MATS = 14

DECAY = 0.1
STEP_SIZE = 0.05
EPSILON = 1e-06

MESH = pl.DeviceIdType.MESH
HALF = 64
CHUNK = 512


def matrix_bounds():
    counts = [QW // TILE, KVW // TILE, KVW // TILE, QW // TILE, NEXP // TILE] + [FF // TILE] * (
        3 * EW
    )
    ends = np.cumsum(counts)
    return [(int(e - c), int(e)) for c, e in zip(counts, ends)]


def select_rows(owner, me, slots):
    tiles = owner.shape[1]
    hit = jnp.broadcast_to((owner == me).astype(jnp.float32), (8, tiles))
    before = (
        lax.broadcasted_iota(jnp.int32, (tiles, tiles), 0)
        < lax.broadcasted_iota(jnp.int32, (tiles, tiles), 1)
    ).astype(jnp.float32)
    rank = jnp.dot(hit, before, preferred_element_type=jnp.float32)
    slot = lax.broadcasted_iota(jnp.int32, (slots, tiles), 0).astype(jnp.float32)
    slot_hit = jnp.where(rank == slot, hit, 0.0)
    lane = lax.broadcasted_iota(jnp.int32, (1, 128), 1) % HALF
    first = jnp.full((1, 128), 1 << 20, jnp.int32)
    last = jnp.zeros((1, 128), jnp.int32)
    for k, (a, b) in enumerate(matrix_bounds()):
        first = jnp.where(lane == k, a, first)
        last = jnp.where(lane == k, b, last)
    tile = lax.broadcasted_iota(jnp.int32, (tiles, 128), 0)
    table = ((tile >= first) & (tile < last)).astype(jnp.float32)
    return jnp.dot(slot_hit, table, preferred_element_type=jnp.float32)


def fold(x):
    x = x[0:8, :] + x[8:16, :]
    out = x[:, 0:128]
    for i in range(1, CHUNK // 128):
        out = out + x[:, i * 128 : (i + 1) * 128]
    return out


def kernel(
    owns, rows,
    w_hbm, f_hbm, s_hbm, g_hbm, owner_hbm,
    nw, nf, ns, low, wn_ref, un_ref, tr_ref,
    wv, fv, sv, gv, dv, owner_ref, used_b, ratio_b, sw, su, abuf, bbuf,
    in_sem, owner_sem, a_sem, b_sem, rs_sem, rr_sem, ls_sem, lr_sem,
):
    own = lax.axis_index("own")
    z = lax.axis_index("row")
    slots, depth, width = wv.shape

    barrier = pltpu.get_barrier_semaphore()

    @pl.loop(1, owns)
    def _(p):
        pl.semaphore_signal(barrier, inc=1, device_id=(lax.rem(own + p, owns), z), device_id_type=MESH)

    @pl.loop(1, rows)
    def _(p):
        pl.semaphore_signal(barrier, inc=1, device_id=(own, lax.rem(z + p, rows)), device_id_type=MESH)

    def loads(c):
        return [
            pltpu.make_async_copy(src.at[0, c], dst.at[c], in_sem.at[i, c])
            for i, (src, dst) in enumerate(((w_hbm, wv), (f_hbm, fv), (s_hbm, sv), (g_hbm, gv)))
        ]

    owner_load = pltpu.make_async_copy(owner_hbm, owner_ref, owner_sem)
    owner_load.start()

    @pl.loop(0, slots)
    def _(c):
        for copy in loads(c):
            copy.start()

    owner_load.wait()
    select = select_rows(owner_ref[...], own, slots)
    lane = lax.broadcasted_iota(jnp.int32, (1, 128), 1)
    lower = lane < HALF
    used = jnp.sum(jnp.where(lower, select, 0.0), axis=1, keepdims=True)
    used_b[...] = jnp.broadcast_to(used, used_b.shape)

    @pl.loop(0, slots)
    def _(c):
        for copy in loads(c):
            copy.wait()
        keep = used_b[pl.ds(c, 1), :]
        aw = jnp.zeros((8, 128), jnp.float32)
        au = jnp.zeros((8, 128), jnp.float32)
        for j in range(width // CHUNK):
            cols = slice(j * CHUNK, (j + 1) * CHUNK)
            w = wv[c, :, cols]
            g = gv[c, :, cols].astype(jnp.float32)
            m1 = 0.5 * fv[c, :, cols] + 0.5 * g
            m2 = 0.5 * sv[c, :, cols] + 0.5 * g * g
            d = m1 / (jnp.sqrt(m2) + EPSILON) + DECAY * w
            nf[0, c, :, cols] = keep * m1
            ns[0, c, :, cols] = keep * m2
            dv[c, :, cols] = d
            aw = aw + fold(w * w)
            au = au + fold(d * d)
        sw[c] = aw
        su[c] = au

    weight_sq = jnp.sum(jnp.sum(sw[...], axis=1), axis=1, keepdims=True)
    update_sq = jnp.sum(jnp.sum(su[...], axis=1), axis=1, keepdims=True)
    part = jnp.sum(select * jnp.where(lower, weight_sq, update_sq), axis=0, keepdims=True)
    abuf[pl.ds(own, 1)] = part.reshape(1, 1, 128)

    pl.semaphore_wait(barrier, owns + rows - 2)

    def plane(p):
        return pltpu.make_async_remote_copy(
            src_ref=abuf.at[own], dst_ref=abuf.at[own],
            send_sem=a_sem.at[0], recv_sem=a_sem.at[1],
            device_id=(lax.rem(own + p, owns), z), device_id_type=MESH,
        )

    def line(p):
        return pltpu.make_async_remote_copy(
            src_ref=bbuf.at[z], dst_ref=bbuf.at[z],
            send_sem=b_sem.at[0], recv_sem=b_sem.at[1],
            device_id=(own, lax.rem(z + p, rows)), device_id_type=MESH,
        )

    @pl.loop(1, owns)
    def _(p):
        plane(p).start()

    whole = abuf.at[pl.ds(0, owns - 1)]
    pltpu.make_async_copy(whole, whole, a_sem.at[1]).wait()
    total = jnp.sum(abuf[...], axis=0)
    bbuf[pl.ds(z, 1)] = total.reshape(1, 1, 128)
    pltpu.make_async_copy(whole, whole, a_sem.at[0]).wait()

    @pl.loop(1, rows)
    def _(p):
        line(p).start()

    whole_b = bbuf.at[pl.ds(0, rows - 1)]
    pltpu.make_async_copy(whole_b, whole_b, b_sem.at[1]).wait()
    norms = jnp.sqrt(jnp.sum(bbuf[...], axis=0))
    updates = pltpu.roll(norms, HALF, 1)
    trust = norms / (updates + EPSILON)
    wn_ref[...] = norms[:, :MATS]
    un_ref[...] = updates[:, :MATS]
    tr_ref[...] = trust[:, :MATS]
    ratio = jnp.sum(jnp.where(lower, select * trust, 0.0), axis=1, keepdims=True)
    ratio_b[...] = jnp.broadcast_to(STEP_SIZE * ratio, ratio_b.shape)

    right, left = lax.rem(z + 1, rows), lax.rem(z + rows - 1, rows)

    def hop(c, h, to_right):
        src = lax.rem(z + rows - h, rows) if to_right else lax.rem(z + h, rows)
        block = low.at[0, c, pl.ds(pl.multiple_of(src * depth, depth), depth)]
        send, recv = (rs_sem, rr_sem) if to_right else (ls_sem, lr_sem)
        return pltpu.make_async_remote_copy(
            src_ref=block, dst_ref=block,
            send_sem=send.at[h, c], recv_sem=recv.at[h, c],
            device_id=(own, right if to_right else left), device_id_type=MESH,
        )

    def arrival(c, h, to_right):
        src = lax.rem(z + rows - h - 1, rows) if to_right else lax.rem(z + h + 1, rows)
        block = low.at[0, c, pl.ds(pl.multiple_of(src * depth, depth), depth)]
        recv = rr_sem if to_right else lr_sem
        pltpu.make_async_copy(block, block, recv.at[h, c]).wait()

    mine = pl.multiple_of(z * depth, depth)

    @pl.loop(0, slots)
    def _(c):
        keep = used_b[pl.ds(c, 1), :]
        rate = ratio_b[pl.ds(c, 1), :]
        for j in range(width // CHUNK):
            cols = slice(j * CHUNK, (j + 1) * CHUNK)
            new = keep * (wv[c, :, cols] - rate * dv[c, :, cols])
            nw[0, c, :, cols] = new
            low[0, c, pl.ds(mine, depth), cols] = new.astype(jnp.bfloat16)
        hop(c, 0, True).start()
        hop(c, 0, False).start()

    half = slots // 2
    far = rows // 2
    for h in range(far):
        last = h == far - 1
        for to_right, lo, hi in ((True, 0, half if last else slots), (False, half if last else 0, slots)):
            @pl.loop(lo, hi)
            def _(c):
                arrival(c, h, to_right)
                if h + 1 < far - 1:
                    hop(c, h + 1, to_right).start()
                elif h + 1 == far - 1:
                    @pl.when((c < half) if to_right else (c >= half))
                    def _():
                        hop(c, h + 1, to_right).start()

    for h in range(far):
        last = h == far - 1
        for to_right, lo, hi in ((True, 0, half if last else slots), (False, half if last else 0, slots)):
            @pl.loop(lo, hi)
            def _(c):
                hop(c, h, to_right).wait_send()

    pltpu.make_async_copy(whole_b, whole_b, b_sem.at[0]).wait()


def put_out(*refs):
    held, result, sem = refs[:7], refs[7:14], refs[14]
    slots = held[0].shape[1]
    copies = []
    for i, (src, dst) in enumerate(zip(held, result)):
        if i == 3:
            copies += [(src.at[0, c], dst.at[0, c]) for c in range(slots)]
        elif i < 3:
            half = slots // 2
            copies += [(src.at[0, pl.ds(c, half)], dst.at[0, pl.ds(c, half)]) for c in (0, half)]
        else:
            copies.append((src, dst))
    copies = [pltpu.make_async_copy(a, b, sem.at[i]) for i, (a, b) in enumerate(copies)]
    for copy in copies:
        copy.start()
    for copy in copies:
        copy.wait()


def shards(owns, rows, weights, first_moment, second_moment, gradient, owner):
    _, slots, depth, width = weights.shape
    hbm = pl.BlockSpec(memory_space=pltpu.HBM)
    vmem = pl.BlockSpec(memory_space=pltpu.VMEM)
    far = rows // 2
    f32 = jnp.float32
    wide = jax.ShapeDtypeStruct(weights.shape, f32)
    tiny = jax.ShapeDtypeStruct((1, MATS), f32)
    dma = pltpu.SemaphoreType.DMA
    result = (
        wide, wide, wide,
        jax.ShapeDtypeStruct((1, slots, depth * rows, width), jnp.bfloat16),
        tiny, tiny, tiny,
    )
    held = pl.pallas_call(
        functools.partial(kernel, owns, rows),
        out_shape=result,
        in_specs=[hbm] * 5,
        out_specs=(vmem,) * 7,
        scratch_shapes=[
            pltpu.VMEM((slots, depth, width), f32),
            pltpu.VMEM((slots, depth, width), f32),
            pltpu.VMEM((slots, depth, width), f32),
            pltpu.VMEM((slots, depth, width), jnp.bfloat16),
            pltpu.VMEM((slots, depth, width), f32),
            pltpu.VMEM((1, owner.shape[0]), jnp.int32),
            pltpu.VMEM((slots, CHUNK), f32),
            pltpu.VMEM((slots, CHUNK), f32),
            pltpu.VMEM((slots, 8, 128), f32),
            pltpu.VMEM((slots, 8, 128), f32),
            pltpu.VMEM((owns, 1, 128), f32),
            pltpu.VMEM((rows, 1, 128), f32),
            dma((4, slots)),
            dma,
            dma((2,)),
            dma((2,)),
            dma((far, slots)),
            dma((far, slots)),
            dma((far, slots)),
            dma((far, slots)),
        ],
        compiler_params=pltpu.CompilerParams(
            collective_id=0, has_side_effects=True, vmem_limit_bytes=24 << 20
        ),
    )(*(pltpu.with_memory_space_constraint(x, pltpu.HBM) for x in (weights, first_moment, second_moment, gradient, owner.reshape(1, -1))))
    nw, nf, ns, low, wn, un, tr = pl.pallas_call(
        put_out,
        out_shape=result,
        in_specs=[vmem] * 7,
        out_specs=(hbm,) * 7,
        scratch_shapes=[dma((slots + 9,))],
        compiler_params=pltpu.CompilerParams(vmem_limit_bytes=24 << 20),
    )(*held)
    return nw, nf, ns, low, wn.reshape(MATS), un.reshape(MATS), tr.reshape(MATS)


def solution(mesh):
    placed = P("own", None, "row", None)
    return jax.shard_map(
        functools.partial(shards, mesh.shape["own"], mesh.shape["row"]),
        mesh=mesh,
        in_specs=(placed, placed, placed, placed, P()),
        out_specs=(placed, placed, placed, P("own", None, None, None), P(), P(), P()),
        check_vma=False,
    )
```

```python
import functools

import jax
import jax.numpy as jnp
import numpy as np
from jax import lax
from jax.experimental import pallas as pl
from jax.experimental.pallas import tpu as pltpu
from jax.sharding import PartitionSpec as P

QW = 4096
KVW = 512
NEXP = 128
FF = 768
EW = 3
TILE = 128
MATS = 14

DECAY = 0.1
STEP_SIZE = 0.05
EPSILON = 1e-06

MESH = pl.DeviceIdType.MESH
HALF = 64
CHUNK = 512


def matrix_bounds():
    counts = [QW // TILE, KVW // TILE, KVW // TILE, QW // TILE, NEXP // TILE] + [FF // TILE] * (
        3 * EW
    )
    ends = np.cumsum(counts)
    return [(int(e - c), int(e)) for c, e in zip(counts, ends)]


def select_rows(owner, me, slots):
    tiles = owner.shape[1]
    hit = jnp.broadcast_to((owner == me).astype(jnp.float32), (8, tiles))
    before = (
        lax.broadcasted_iota(jnp.int32, (tiles, tiles), 0)
        < lax.broadcasted_iota(jnp.int32, (tiles, tiles), 1)
    ).astype(jnp.float32)
    rank = jnp.dot(hit, before, preferred_element_type=jnp.float32)
    slot = lax.broadcasted_iota(jnp.int32, (slots, tiles), 0).astype(jnp.float32)
    slot_hit = jnp.where(rank == slot, hit, 0.0)
    lane = lax.broadcasted_iota(jnp.int32, (1, 128), 1) % HALF
    first = jnp.full((1, 128), 1 << 20, jnp.int32)
    last = jnp.zeros((1, 128), jnp.int32)
    for k, (a, b) in enumerate(matrix_bounds()):
        first = jnp.where(lane == k, a, first)
        last = jnp.where(lane == k, b, last)
    tile = lax.broadcasted_iota(jnp.int32, (tiles, 128), 0)
    table = ((tile >= first) & (tile < last)).astype(jnp.float32)
    return jnp.dot(slot_hit, table, preferred_element_type=jnp.float32)


def fold(x):
    x = x[0:8, :] + x[8:16, :]
    out = x[:, 0:128]
    for i in range(1, CHUNK // 128):
        out = out + x[:, i * 128 : (i + 1) * 128]
    return out


def pick_plan(plans, owns, owner_ref, plan_ref):
    tiles = owner_ref.shape[1]
    group = lax.broadcasted_iota(jnp.int32, (owns, tiles), 0)
    hit = (jnp.broadcast_to(owner_ref[...], (owns, tiles)) == group).astype(jnp.float32)
    counts = jnp.broadcast_to(jnp.sum(hit, axis=1, keepdims=True), (owns, 128))
    odd = lax.broadcasted_iota(jnp.int32, (owns, 128), 0) % 2 == 1
    most_even = jnp.max(jnp.where(odd, 0.0, counts)).astype(jnp.int32)
    most_odd = jnp.max(jnp.where(odd, counts, 0.0)).astype(jnp.int32)
    plan = jnp.int32(0)
    for i, (even, odd_slots) in enumerate(plans):
        plan = jnp.where((most_even <= even) & (most_odd <= odd_slots), i, plan)
    plan_ref[0] = plan


def kernel(
    owns, rows, sent,
    w_hbm, f_hbm, s_hbm, g_hbm, owner_hbm,
    nw, nf, ns, low, wn_ref, un_ref, tr_ref,
    wv, fv, sv, gv, dv, owner_ref, used_b, ratio_b, sw, su, abuf, bbuf,
    in_sem, owner_sem, a_sem, b_sem, rs_sem, rr_sem, ls_sem, lr_sem,
):
    own = lax.axis_index("own")
    z = lax.axis_index("row")
    slots, depth, width = wv.shape

    count = sent[0] + (sent[1] - sent[0]) * lax.rem(own, 2)

    barrier = pltpu.get_barrier_semaphore()

    @pl.loop(1, owns)
    def _(p):
        pl.semaphore_signal(barrier, inc=1, device_id=(lax.rem(own + p, owns), z), device_id_type=MESH)

    @pl.loop(1, rows)
    def _(p):
        pl.semaphore_signal(barrier, inc=1, device_id=(own, lax.rem(z + p, rows)), device_id_type=MESH)

    def loads(c):
        return [
            pltpu.make_async_copy(src.at[0, c], dst.at[c], in_sem.at[i, c])
            for i, (src, dst) in enumerate(((w_hbm, wv), (f_hbm, fv), (s_hbm, sv), (g_hbm, gv)))
        ]

    owner_load = pltpu.make_async_copy(owner_hbm, owner_ref, owner_sem)
    owner_load.start()

    @pl.loop(0, slots)
    def _(c):
        for copy in loads(c):
            copy.start()

    owner_load.wait()
    select = select_rows(owner_ref[...], own, slots)
    lane = lax.broadcasted_iota(jnp.int32, (1, 128), 1)
    lower = lane < HALF
    used = jnp.sum(jnp.where(lower, select, 0.0), axis=1, keepdims=True)
    used_b[...] = jnp.broadcast_to(used, used_b.shape)

    @pl.loop(0, slots)
    def _(c):
        for copy in loads(c):
            copy.wait()
        keep = used_b[pl.ds(c, 1), :]
        aw = jnp.zeros((8, 128), jnp.float32)
        au = jnp.zeros((8, 128), jnp.float32)
        for j in range(width // CHUNK):
            cols = slice(j * CHUNK, (j + 1) * CHUNK)
            w = wv[c, :, cols]
            g = gv[c, :, cols].astype(jnp.float32)
            m1 = 0.5 * fv[c, :, cols] + 0.5 * g
            m2 = 0.5 * sv[c, :, cols] + 0.5 * g * g
            d = m1 / (jnp.sqrt(m2) + EPSILON) + DECAY * w
            nf[0, c, :, cols] = keep * m1
            ns[0, c, :, cols] = keep * m2
            dv[c, :, cols] = d
            aw = aw + fold(w * w)
            au = au + fold(d * d)
        sw[c] = aw
        su[c] = au

    weight_sq = jnp.sum(jnp.sum(sw[...], axis=1), axis=1, keepdims=True)
    update_sq = jnp.sum(jnp.sum(su[...], axis=1), axis=1, keepdims=True)
    part = jnp.sum(select * jnp.where(lower, weight_sq, update_sq), axis=0, keepdims=True)
    abuf[pl.ds(own, 1)] = part.reshape(1, 1, 128)

    pl.semaphore_wait(barrier, owns + rows - 2)

    def plane(p):
        return pltpu.make_async_remote_copy(
            src_ref=abuf.at[own], dst_ref=abuf.at[own],
            send_sem=a_sem.at[0], recv_sem=a_sem.at[1],
            device_id=(lax.rem(own + p, owns), z), device_id_type=MESH,
        )

    def line(p):
        return pltpu.make_async_remote_copy(
            src_ref=bbuf.at[z], dst_ref=bbuf.at[z],
            send_sem=b_sem.at[0], recv_sem=b_sem.at[1],
            device_id=(own, lax.rem(z + p, rows)), device_id_type=MESH,
        )

    @pl.loop(1, owns)
    def _(p):
        plane(p).start()

    @pl.loop(count, slots)
    def _(c):
        low[0, c] = jnp.zeros(low.shape[2:], low.dtype)

    whole = abuf.at[pl.ds(0, owns - 1)]
    pltpu.make_async_copy(whole, whole, a_sem.at[1]).wait()
    total = jnp.sum(abuf[...], axis=0)
    bbuf[pl.ds(z, 1)] = total.reshape(1, 1, 128)
    pltpu.make_async_copy(whole, whole, a_sem.at[0]).wait()

    @pl.loop(1, rows)
    def _(p):
        line(p).start()

    whole_b = bbuf.at[pl.ds(0, rows - 1)]
    pltpu.make_async_copy(whole_b, whole_b, b_sem.at[1]).wait()
    norms = jnp.sqrt(jnp.sum(bbuf[...], axis=0))
    updates = pltpu.roll(norms, HALF, 1)
    trust = norms / (updates + EPSILON)
    wn_ref[...] = norms[:, :MATS]
    un_ref[...] = updates[:, :MATS]
    tr_ref[...] = trust[:, :MATS]
    ratio = jnp.sum(jnp.where(lower, select * trust, 0.0), axis=1, keepdims=True)
    ratio_b[...] = jnp.broadcast_to(STEP_SIZE * ratio, ratio_b.shape)

    right, left = lax.rem(z + 1, rows), lax.rem(z + rows - 1, rows)
    far = rows // 2

    def piece(c, src, h, to_right):
        block = low.at[0, c, pl.ds(pl.multiple_of(src * depth, depth), depth)]
        if h < far - 1:
            return block
        return block.at[:, pl.ds(0 if to_right else width // 2, width // 2)]

    def hop(c, h, to_right):
        src = lax.rem(z + rows - h, rows) if to_right else lax.rem(z + h, rows)
        block = piece(c, src, h, to_right)
        send, recv = (rs_sem, rr_sem) if to_right else (ls_sem, lr_sem)
        return pltpu.make_async_remote_copy(
            src_ref=block, dst_ref=block,
            send_sem=send.at[h, c], recv_sem=recv.at[h, c],
            device_id=(own, right if to_right else left), device_id_type=MESH,
        )

    def arrival(c, h, to_right):
        src = lax.rem(z + rows - h - 1, rows) if to_right else lax.rem(z + h + 1, rows)
        block = piece(c, src, h, to_right)
        recv = rr_sem if to_right else lr_sem
        pltpu.make_async_copy(block, block, recv.at[h, c]).wait()

    mine = pl.multiple_of(z * depth, depth)

    @pl.loop(0, slots)
    def _(c):
        keep = used_b[pl.ds(c, 1), :]
        rate = ratio_b[pl.ds(c, 1), :]
        for j in range(width // CHUNK):
            cols = slice(j * CHUNK, (j + 1) * CHUNK)
            new = keep * (wv[c, :, cols] - rate * dv[c, :, cols])
            nw[0, c, :, cols] = new
            low[0, c, pl.ds(mine, depth), cols] = new.astype(jnp.bfloat16)

        @pl.when(c < count)
        def _():
            hop(c, 0, True).start()
            hop(c, 0, False).start()

    for h in range(far):
        @pl.loop(0, count)
        def _(c):
            for to_right in (True, False):
                arrival(c, h, to_right)
                if h + 1 < far:
                    hop(c, h + 1, to_right).start()

    for h in range(far):
        @pl.loop(0, count)
        def _(c):
            for to_right in (True, False):
                hop(c, h, to_right).wait_send()

    pltpu.make_async_copy(whole_b, whole_b, b_sem.at[0]).wait()


def put_out(*refs):
    held, result, sem = refs[:7], refs[7:14], refs[14]
    slots = held[0].shape[1]
    copies = []
    for i, (src, dst) in enumerate(zip(held, result)):
        if i == 3:
            copies += [(src.at[0, c], dst.at[0, c]) for c in range(slots)]
        elif i < 3:
            half = slots // 2
            copies += [(src.at[0, pl.ds(c, half)], dst.at[0, pl.ds(c, half)]) for c in (0, half)]
        else:
            copies.append((src, dst))
    copies = [pltpu.make_async_copy(a, b, sem.at[i]) for i, (a, b) in enumerate(copies)]
    for copy in copies:
        copy.start()
    for copy in copies:
        copy.wait()


def update(owns, rows, number, sent, weights, first_moment, second_moment, gradient, owner):
    _, slots, depth, width = weights.shape
    hbm = pl.BlockSpec(memory_space=pltpu.HBM)
    vmem = pl.BlockSpec(memory_space=pltpu.VMEM)
    far = rows // 2
    f32 = jnp.float32
    wide = jax.ShapeDtypeStruct(weights.shape, f32)
    tiny = jax.ShapeDtypeStruct((1, MATS), f32)
    dma = pltpu.SemaphoreType.DMA
    result = (
        wide, wide, wide,
        jax.ShapeDtypeStruct((1, slots, depth * rows, width), jnp.bfloat16),
        tiny, tiny, tiny,
    )
    held = pl.pallas_call(
        functools.partial(kernel, owns, rows, sent),
        out_shape=result,
        in_specs=[hbm] * 5,
        out_specs=(vmem,) * 7,
        scratch_shapes=[
            pltpu.VMEM((slots, depth, width), f32),
            pltpu.VMEM((slots, depth, width), f32),
            pltpu.VMEM((slots, depth, width), f32),
            pltpu.VMEM((slots, depth, width), jnp.bfloat16),
            pltpu.VMEM((slots, depth, width), f32),
            pltpu.VMEM((1, owner.shape[0]), jnp.int32),
            pltpu.VMEM((slots, CHUNK), f32),
            pltpu.VMEM((slots, CHUNK), f32),
            pltpu.VMEM((slots, 8, 128), f32),
            pltpu.VMEM((slots, 8, 128), f32),
            pltpu.VMEM((owns, 1, 128), f32),
            pltpu.VMEM((rows, 1, 128), f32),
            dma((4, slots)),
            dma,
            dma((2,)),
            dma((2,)),
            dma((far, slots)),
            dma((far, slots)),
            dma((far, slots)),
            dma((far, slots)),
        ],
        compiler_params=pltpu.CompilerParams(
            collective_id=number, has_side_effects=True, vmem_limit_bytes=24 << 20
        ),
    )(*(pltpu.with_memory_space_constraint(x, pltpu.HBM) for x in (weights, first_moment, second_moment, gradient, owner.reshape(1, -1))))
    nw, nf, ns, low, wn, un, tr = pl.pallas_call(
        put_out,
        out_shape=result,
        in_specs=[vmem] * 7,
        out_specs=(hbm,) * 7,
        scratch_shapes=[dma((slots + 9,))],
        compiler_params=pltpu.CompilerParams(vmem_limit_bytes=24 << 20),
    )(*held)
    return nw, nf, ns, low, wn.reshape(MATS), un.reshape(MATS), tr.reshape(MATS)


def shards(owns, rows, *arrays):
    slots, owner = arrays[0].shape[1], arrays[-1]
    plans = [(slots, slots), (slots, slots // 2), (slots // 2, slots)]
    plan = pl.pallas_call(
        functools.partial(pick_plan, plans, owns),
        out_shape=jax.ShapeDtypeStruct((1,), jnp.int32),
        in_specs=[pl.BlockSpec(memory_space=pltpu.VMEM)],
        out_specs=pl.BlockSpec(memory_space=pltpu.SMEM),
    )(owner.reshape(1, -1))
    branches = [functools.partial(update, owns, rows, i, sent) for i, sent in enumerate(plans)]
    return lax.switch(plan[0], branches, *arrays)


def solution(mesh):
    placed = P("own", None, "row", None)
    return jax.shard_map(
        functools.partial(shards, mesh.shape["own"], mesh.shape["row"]),
        mesh=mesh,
        in_specs=(placed, placed, placed, placed, P()),
        out_specs=(placed, placed, placed, P("own", None, None, None), P(), P(), P()),
        check_vma=False,
    )
```

```python
import functools

import jax
import jax.numpy as jnp
import numpy as np
from jax import lax
from jax.experimental import pallas as pl
from jax.experimental.pallas import tpu as pltpu
from jax.sharding import PartitionSpec as P

QW = 4096
KVW = 512
NEXP = 128
FF = 768
EW = 3
TILE = 128
MATS = 14

DECAY = 0.1
STEP_SIZE = 0.05
EPSILON = 1e-06

MESH = pl.DeviceIdType.MESH
HALF = 64
CHUNK = 512


def matrix_bounds():
    counts = [QW // TILE, KVW // TILE, KVW // TILE, QW // TILE, NEXP // TILE] + [FF // TILE] * (
        3 * EW
    )
    ends = np.cumsum(counts)
    return [(int(e - c), int(e)) for c, e in zip(counts, ends)]


def select_rows(owner, me, slots):
    tiles = owner.shape[1]
    hit = jnp.broadcast_to((owner == me).astype(jnp.float32), (8, tiles))
    before = (
        lax.broadcasted_iota(jnp.int32, (tiles, tiles), 0)
        < lax.broadcasted_iota(jnp.int32, (tiles, tiles), 1)
    ).astype(jnp.float32)
    rank = jnp.dot(hit, before, preferred_element_type=jnp.float32)
    slot = lax.broadcasted_iota(jnp.int32, (slots, tiles), 0).astype(jnp.float32)
    slot_hit = jnp.where(rank == slot, hit, 0.0)
    lane = lax.broadcasted_iota(jnp.int32, (1, 128), 1) % HALF
    first = jnp.full((1, 128), 1 << 20, jnp.int32)
    last = jnp.zeros((1, 128), jnp.int32)
    for k, (a, b) in enumerate(matrix_bounds()):
        first = jnp.where(lane == k, a, first)
        last = jnp.where(lane == k, b, last)
    tile = lax.broadcasted_iota(jnp.int32, (tiles, 128), 0)
    table = ((tile >= first) & (tile < last)).astype(jnp.float32)
    return jnp.dot(slot_hit, table, preferred_element_type=jnp.float32)


def fold(x):
    x = x[0:8, :] + x[8:16, :]
    out = x[:, 0:128]
    for i in range(1, CHUNK // 128):
        out = out + x[:, i * 128 : (i + 1) * 128]
    return out


def pick_plan(plans, owns, owner_ref, plan_ref):
    tiles = owner_ref.shape[1]
    group = lax.broadcasted_iota(jnp.int32, (owns, tiles), 0)
    hit = (jnp.broadcast_to(owner_ref[...], (owns, tiles)) == group).astype(jnp.float32)
    counts = jnp.broadcast_to(jnp.sum(hit, axis=1, keepdims=True), (owns, 128))
    odd = lax.broadcasted_iota(jnp.int32, (owns, 128), 0) % 2 == 1
    most_even = jnp.max(jnp.where(odd, 0.0, counts)).astype(jnp.int32)
    most_odd = jnp.max(jnp.where(odd, counts, 0.0)).astype(jnp.int32)
    plan = jnp.int32(0)
    for i, (even, odd_slots) in enumerate(plans):
        plan = jnp.where((most_even <= even) & (most_odd <= odd_slots), i, plan)
    plan_ref[0] = plan


def kernel(
    owns, rows, sent,
    w_hbm, f_hbm, s_hbm, g_hbm, owner_hbm,
    nw, nf, ns, low, wn_ref, un_ref, tr_ref,
    wv, fv, sv, gv, dv, owner_ref, used_b, ratio_b, sw, su, abuf, bbuf,
    in_sem, owner_sem, a_sem, b_sem, rs_sem, rr_sem, ls_sem, lr_sem,
):
    own = lax.axis_index("own")
    z = lax.axis_index("row")
    slots, depth, width = wv.shape

    count = sent[0] + (sent[1] - sent[0]) * lax.rem(own, 2)

    barrier = pltpu.get_barrier_semaphore()

    @pl.loop(1, owns)
    def _(p):
        pl.semaphore_signal(barrier, inc=1, device_id=(lax.rem(own + p, owns), z), device_id_type=MESH)

    @pl.loop(1, rows)
    def _(p):
        pl.semaphore_signal(barrier, inc=1, device_id=(own, lax.rem(z + p, rows)), device_id_type=MESH)

    def loads(c):
        return [
            pltpu.make_async_copy(src.at[0, c], dst.at[c], in_sem.at[i, c])
            for i, (src, dst) in enumerate(((w_hbm, wv), (f_hbm, fv), (s_hbm, sv), (g_hbm, gv)))
        ]

    owner_load = pltpu.make_async_copy(owner_hbm, owner_ref, owner_sem)
    owner_load.start()

    @pl.loop(0, slots)
    def _(c):
        for copy in loads(c):
            copy.start()

    owner_load.wait()
    select = select_rows(owner_ref[...], own, slots)
    lane = lax.broadcasted_iota(jnp.int32, (1, 128), 1)
    lower = lane < HALF
    used = jnp.sum(jnp.where(lower, select, 0.0), axis=1, keepdims=True)
    used_b[...] = jnp.broadcast_to(used, used_b.shape)

    @pl.loop(0, slots)
    def _(c):
        for copy in loads(c):
            copy.wait()
        keep = used_b[pl.ds(c, 1), :]
        aw = jnp.zeros((8, 128), jnp.float32)
        au = jnp.zeros((8, 128), jnp.float32)
        for j in range(width // CHUNK):
            cols = slice(j * CHUNK, (j + 1) * CHUNK)
            w = wv[c, :, cols]
            g = gv[c, :, cols].astype(jnp.float32)
            m1 = 0.5 * fv[c, :, cols] + 0.5 * g
            m2 = 0.5 * sv[c, :, cols] + 0.5 * g * g
            d = m1 / (jnp.sqrt(m2) + EPSILON) + DECAY * w
            nf[0, c, :, cols] = keep * m1
            ns[0, c, :, cols] = keep * m2
            dv[c, :, cols] = d
            aw = aw + fold(w * w)
            au = au + fold(d * d)
        sw[c] = aw
        su[c] = au

    weight_sq = jnp.sum(jnp.sum(sw[...], axis=1), axis=1, keepdims=True)
    update_sq = jnp.sum(jnp.sum(su[...], axis=1), axis=1, keepdims=True)
    part = jnp.sum(select * jnp.where(lower, weight_sq, update_sq), axis=0, keepdims=True)
    abuf[pl.ds(own, 1)] = part.reshape(1, 1, 128)

    pl.semaphore_wait(barrier, owns + rows - 2)

    def plane(p):
        return pltpu.make_async_remote_copy(
            src_ref=abuf.at[own], dst_ref=abuf.at[own],
            send_sem=a_sem.at[0], recv_sem=a_sem.at[1],
            device_id=(lax.rem(own + p, owns), z), device_id_type=MESH,
        )

    def line(p):
        return pltpu.make_async_remote_copy(
            src_ref=bbuf.at[z], dst_ref=bbuf.at[z],
            send_sem=b_sem.at[0], recv_sem=b_sem.at[1],
            device_id=(own, lax.rem(z + p, rows)), device_id_type=MESH,
        )

    @pl.loop(1, owns)
    def _(p):
        plane(p).start()

    @pl.loop(count, slots)
    def _(c):
        low[0, c] = jnp.zeros(low.shape[2:], low.dtype)

    whole = abuf.at[pl.ds(0, owns - 1)]
    pltpu.make_async_copy(whole, whole, a_sem.at[1]).wait()
    total = jnp.sum(abuf[...], axis=0)
    bbuf[pl.ds(z, 1)] = total.reshape(1, 1, 128)

    @pl.loop(1, rows)
    def _(p):
        line(p).start()

    whole_b = bbuf.at[pl.ds(0, rows - 1)]
    pltpu.make_async_copy(whole_b, whole_b, b_sem.at[1]).wait()
    norms = jnp.sqrt(jnp.sum(bbuf[...], axis=0))
    updates = pltpu.roll(norms, HALF, 1)
    trust = norms / (updates + EPSILON)
    wn_ref[...] = norms[:, :MATS]
    un_ref[...] = updates[:, :MATS]
    tr_ref[...] = trust[:, :MATS]
    ratio = jnp.sum(jnp.where(lower, select * trust, 0.0), axis=1, keepdims=True)
    ratio_b[...] = jnp.broadcast_to(STEP_SIZE * ratio, ratio_b.shape)

    right, left = lax.rem(z + 1, rows), lax.rem(z + rows - 1, rows)
    far = rows // 2

    def piece(c, src, h, to_right):
        block = low.at[0, c, pl.ds(pl.multiple_of(src * depth, depth), depth)]
        if h < far - 1:
            return block
        return block.at[:, pl.ds(0 if to_right else width // 2, width // 2)]

    def hop(c, h, to_right):
        src = lax.rem(z + rows - h, rows) if to_right else lax.rem(z + h, rows)
        block = piece(c, src, h, to_right)
        send, recv = (rs_sem, rr_sem) if to_right else (ls_sem, lr_sem)
        return pltpu.make_async_remote_copy(
            src_ref=block, dst_ref=block,
            send_sem=send.at[h, c], recv_sem=recv.at[h, c],
            device_id=(own, right if to_right else left), device_id_type=MESH,
        )

    def arrival(c, h, to_right):
        src = lax.rem(z + rows - h - 1, rows) if to_right else lax.rem(z + h + 1, rows)
        block = piece(c, src, h, to_right)
        recv = rr_sem if to_right else lr_sem
        pltpu.make_async_copy(block, block, recv.at[h, c]).wait()

    mine = pl.multiple_of(z * depth, depth)

    @pl.loop(0, slots)
    def _(c):
        keep = used_b[pl.ds(c, 1), :]
        rate = ratio_b[pl.ds(c, 1), :]
        for j in range(width // CHUNK):
            cols = slice(j * CHUNK, (j + 1) * CHUNK)
            new = keep * (wv[c, :, cols] - rate * dv[c, :, cols])
            nw[0, c, :, cols] = new
            low[0, c, pl.ds(mine, depth), cols] = new.astype(jnp.bfloat16)

        @pl.when(c < count)
        def _():
            hop(c, 0, True).start()
            hop(c, 0, False).start()

    for h in range(far):
        @pl.loop(0, count)
        def _(c):
            for to_right in (True, False):
                arrival(c, h, to_right)
                if h + 1 < far:
                    hop(c, h + 1, to_right).start()

    for h in range(far):
        @pl.loop(0, count)
        def _(c):
            for to_right in (True, False):
                hop(c, h, to_right).wait_send()

    pltpu.make_async_copy(whole, whole, a_sem.at[0]).wait()
    pltpu.make_async_copy(whole_b, whole_b, b_sem.at[0]).wait()


def put_out(*refs):
    held, result, sem = refs[:7], refs[7:14], refs[14]
    slots = held[0].shape[1]
    copies = []
    for i, (src, dst) in enumerate(zip(held, result)):
        if i == 3:
            copies += [(src.at[0, c], dst.at[0, c]) for c in range(slots)]
        elif i < 3:
            half = slots // 2
            copies += [(src.at[0, pl.ds(c, half)], dst.at[0, pl.ds(c, half)]) for c in (0, half)]
        else:
            copies.append((src, dst))
    copies = [pltpu.make_async_copy(a, b, sem.at[i]) for i, (a, b) in enumerate(copies)]
    for copy in copies:
        copy.start()
    for copy in copies:
        copy.wait()


def update(owns, rows, number, sent, weights, first_moment, second_moment, gradient, owner):
    _, slots, depth, width = weights.shape
    hbm = pl.BlockSpec(memory_space=pltpu.HBM)
    vmem = pl.BlockSpec(memory_space=pltpu.VMEM)
    far = rows // 2
    f32 = jnp.float32
    wide = jax.ShapeDtypeStruct(weights.shape, f32)
    tiny = jax.ShapeDtypeStruct((1, MATS), f32)
    dma = pltpu.SemaphoreType.DMA
    result = (
        wide, wide, wide,
        jax.ShapeDtypeStruct((1, slots, depth * rows, width), jnp.bfloat16),
        tiny, tiny, tiny,
    )
    held = pl.pallas_call(
        functools.partial(kernel, owns, rows, sent),
        out_shape=result,
        in_specs=[hbm] * 5,
        out_specs=(vmem,) * 7,
        scratch_shapes=[
            pltpu.VMEM((slots, depth, width), f32),
            pltpu.VMEM((slots, depth, width), f32),
            pltpu.VMEM((slots, depth, width), f32),
            pltpu.VMEM((slots, depth, width), jnp.bfloat16),
            pltpu.VMEM((slots, depth, width), f32),
            pltpu.VMEM((1, owner.shape[0]), jnp.int32),
            pltpu.VMEM((slots, CHUNK), f32),
            pltpu.VMEM((slots, CHUNK), f32),
            pltpu.VMEM((slots, 8, 128), f32),
            pltpu.VMEM((slots, 8, 128), f32),
            pltpu.VMEM((owns, 1, 128), f32),
            pltpu.VMEM((rows, 1, 128), f32),
            dma((4, slots)),
            dma,
            dma((2,)),
            dma((2,)),
            dma((far, slots)),
            dma((far, slots)),
            dma((far, slots)),
            dma((far, slots)),
        ],
        compiler_params=pltpu.CompilerParams(
            collective_id=number, has_side_effects=True, vmem_limit_bytes=24 << 20
        ),
    )(*(pltpu.with_memory_space_constraint(x, pltpu.HBM) for x in (weights, first_moment, second_moment, gradient, owner.reshape(1, -1))))
    nw, nf, ns, low, wn, un, tr = pl.pallas_call(
        put_out,
        out_shape=result,
        in_specs=[vmem] * 7,
        out_specs=(hbm,) * 7,
        scratch_shapes=[dma((slots + 9,))],
        compiler_params=pltpu.CompilerParams(vmem_limit_bytes=24 << 20),
    )(*held)
    return nw, nf, ns, low, wn.reshape(MATS), un.reshape(MATS), tr.reshape(MATS)


def shards(owns, rows, *arrays):
    slots, owner = arrays[0].shape[1], arrays[-1]
    plans = [(slots, slots), (slots, slots // 2), (slots // 2, slots)]
    plan = pl.pallas_call(
        functools.partial(pick_plan, plans, owns),
        out_shape=jax.ShapeDtypeStruct((1,), jnp.int32),
        in_specs=[pl.BlockSpec(memory_space=pltpu.VMEM)],
        out_specs=pl.BlockSpec(memory_space=pltpu.SMEM),
    )(owner.reshape(1, -1))
    branches = [functools.partial(update, owns, rows, i, sent) for i, sent in enumerate(plans)]
    return lax.switch(plan[0], branches, *arrays)


def solution(mesh):
    placed = P("own", None, "row", None)
    return jax.shard_map(
        functools.partial(shards, mesh.shape["own"], mesh.shape["row"]),
        mesh=mesh,
        in_specs=(placed, placed, placed, placed, P()),
        out_specs=(placed, placed, placed, P("own", None, None, None), P(), P(), P()),
        check_vma=False,
    )
```
